32 devices in a mesh: section: 4 (over y, x), dp: 8 (over z, core).
Axes of the slice: x: 2, y: 2, z: 4, core: 2. Of those that a mesh axis runs over, the one named last changes fastest.
Arguments:
- hidden: bfloat16 [512, 4096], P('dp'), may hold values from -6 to 6
- neighbours: bfloat16 [8, 128, 4096], P('dp'), may hold values from -28 to 28
- norm_gain: float32 [4, 4096], P('section'), may hold values from 0.5 to 2
- w_query: bfloat16 [4, 4096, 4096], P('section', None, 'dp'), may hold values from -0.09375 to 0.09375
- w_kv: bfloat16 [4, 4096, 2, 4096], P('section', None, None, 'dp'), may hold values from -0.09375 to 0.09375
- w_out: bfloat16 [4, 4096, 4096], P('section', 'dp'), may hold values from -0.375 to 0.375
Outputs:
- section_outputs: bfloat16 [4, 512, 4096], P('section', 'dp')
The draws below stay inside these ranges and needn't reach their ends.
All inputs are finite; a program needn't handle non-finite values.
Results may differ from the reference program's by a relative error of at most 0.03.
The reference program's roundings to bfloat16 on the way count: a program that leaves them out, or rounds other values in their place, can miss the bound.
Values may be sent and summed in bfloat16 or wider, within the bound.
A program may use at most 128 MiB of HBM per device.

```python
import math
import jax
import jax.numpy as jnp
from jax import lax

D = 4096
HEADS = 32
DH = 128
BLOCK_LEN = 64
NLEN = 128
HD = 4096
HG = 4
TOKENS = 512
N_SECTION = 4
N_DP = 8


def weight_block(key, salt):
    raw_normal = jax.random.normal(jax.random.fold_in(key, salt), (N_SECTION, D, HD), jnp.float32)
    return jnp.clip(raw_normal, -6.0, 6.0) * D ** (-0.5)


def draw_w_query(key, part):
    return weight_block(key, 101).astype(jnp.bfloat16)


def draw_w_kv(key, part):
    key_part = weight_block(key, 102)
    value_part = weight_block(key, 103)
    return jnp.stack([key_part, value_part], axis=2).astype(jnp.bfloat16)


def draw_hidden(key, part):
    drawn_rows = jnp.clip(jax.random.normal(jax.random.fold_in(key, 301), (TOKENS, D), jnp.float32), -6.0, 6.0)
    return drawn_rows.astype(jnp.bfloat16)


def draw_neighbours(key, part):
    block_total = TOKENS // BLOCK_LEN
    drawn_rows = jnp.clip(jax.random.normal(jax.random.fold_in(key, 401), (block_total, NLEN, D), jnp.float32), -6.0, 6.0)
    return drawn_rows.astype(jnp.bfloat16)


def block_levels(key, dims, cuts, smallest, high):
    factor_of, own = 1.0, jax.random.fold_in(key, 6)
    for axis_at, blocks in cuts:
        heights = jnp.exp(jax.random.uniform(jax.random.fold_in(own, axis_at), (blocks,), jnp.float32, smallest / len(cuts), high / len(cuts)))
        factor_of = factor_of * jnp.repeat(heights, dims[axis_at] // blocks).reshape([-1 if axis == axis_at else 1 for axis in range(len(dims))])
    return factor_of


def noise(key, extent, spread, limit, cuts=(), dtype=jnp.bfloat16):
    entries = jax.random.normal(key, extent, jnp.float32) * spread
    if len(cuts) > 0:
        entries = block_levels(key, extent, cuts, -0.22, 0.18) * entries
    return jnp.clip(entries, min=-limit, max=limit).astype(dtype)


def setup_inputs(seed: int = 0) -> dict:
    splits = jax.random.split(jax.random.key(seed), 7)
    return {
        "hidden": draw_hidden(jax.random.fold_in(splits[6], 71), 0),
        "neighbours": draw_neighbours(jax.random.fold_in(splits[6], 71), 0),
        "norm_gain": jnp.clip(jnp.exp(math.log(2.0) - 1.3862944 * jax.random.uniform(splits[2], (N_SECTION, D), jnp.float32) ** block_levels(splits[2], (N_SECTION, D), ((0, 4),), -0.2, 0.2)), 0.5, 2.0),
        "w_query": draw_w_query(jax.random.fold_in(splits[6], 71), 0),
        "w_kv": draw_w_kv(jax.random.fold_in(splits[6], 71), 0),
        "w_out": noise(splits[5], (N_SECTION, HD, D), (HD // 16) ** -0.5, 0.375, ((0, 4), (1, 8))),
    }


def reference(hidden, neighbours, norm_gain, w_query, w_kv, w_out):
    groups_all = TOKENS // BLOCK_LEN
    group_width = HG * DH
    scaling = DH ** (-0.5)
    current = hidden
    results = []
    for section_number in range(N_SECTION):
        widened = current.astype(jnp.float32)
        moment = lax.optimization_barrier(jnp.mean(widened * widened, axis=-1, keepdims=True))
        normed = (widened * lax.rsqrt(moment + 1e-05) * norm_gain[section_number]).astype(jnp.bfloat16)
        queries = (jnp.dot(normed, w_query[section_number], preferred_element_type=jnp.float32) * scaling).astype(jnp.bfloat16)
        flat_neighbours = neighbours.reshape(groups_all * NLEN, D)
        projected = jnp.dot(flat_neighbours, w_kv[section_number].reshape(D, 2 * HEADS * DH), preferred_element_type=jnp.float32).astype(jnp.bfloat16)
        projected = projected.reshape(groups_all, NLEN, 2, HEADS, DH)
        keys_all = projected[:, :, 0].astype(jnp.float32)
        values_all = projected[:, :, 1].astype(jnp.float32)
        query_blocks = queries.reshape(groups_all, BLOCK_LEN, HEADS, DH).astype(jnp.float32)
        scores = jnp.einsum('gqhe,gkhe->ghqk', query_blocks, keys_all)
        weights_soft = jax.nn.softmax(scores, axis=-1).astype(jnp.bfloat16)
        attended = jnp.einsum('ghqk,gkhe->gqhe', weights_soft.astype(jnp.float32), values_all).astype(jnp.bfloat16)
        attended = attended.reshape(TOKENS, HEADS * DH)
        running = widened
        for group_number in range(N_DP):
            group_cols = attended[:, group_number * group_width:(group_number + 1) * group_width]
            group_rows = w_out[section_number, group_number * group_width:(group_number + 1) * group_width]
            partial_term = jnp.dot(group_cols, group_rows, preferred_element_type=jnp.float32).astype(jnp.bfloat16)
            running = running + lax.optimization_barrier(partial_term).astype(jnp.float32)
        current = running.astype(jnp.bfloat16)
        results.append(current)
    return jnp.stack(results)
```

```python
import functools
import jax
import jax.numpy as jnp
from jax import lax
from jax.experimental import pallas as pl
from jax.experimental.pallas import tpu as pltpu
from jax.sharding import PartitionSpec as P

DH = 128
BLOCK_LEN = 64
MB = 16
CHUNKS = 2
F32 = jnp.float32
BF16 = jnp.bfloat16


def remote(src, dst, send_sem, recv_sem, section, dp):
    return pltpu.make_async_remote_copy(
        src_ref=src,
        dst_ref=dst,
        send_sem=send_sem,
        recv_sem=recv_sem,
        device_id=(section, dp),
        device_id_type=pl.DeviceIdType.MESH,
    )


def relay_kernel(
    sections,
    group,
    hidden_hbm,
    gain_ref,
    wq_hbm,
    kv_ref,
    wo_hbm,
    out_ref,
    wq,
    wo,
    hbuf,
    gbuf,
    pbuf,
    r1,
    tsum,
    r2,
    load_sem,
    h_send,
    h_recv,
    g_send,
    g_recv,
    f_send,
    f_recv,
    r1_send,
    r1_recv,
    r2_send,
    r2_recv,
):
    section = lax.axis_index("section")
    me = lax.axis_index("dp")
    chips = group // 2
    core = me % 2
    chip = me // 2
    other = 1 - core
    sibling = chip * 2 + other
    micro_count, mb, features = hbuf.shape
    cols = wq.shape[1]
    heads = cols // DH
    per_dev = kv_ref.shape[0] // group
    width = features // CHUNKS
    scaling = DH ** (-0.5)

    def peer(k):
        return ((chip + k) % chips) * 2 + core

    def source_chip(k):
        return (chip + chips - k) % chips

    wq_load = pltpu.make_async_copy(wq_hbm, wq, load_sem.at[0])
    wo_load = pltpu.make_async_copy(wo_hbm, wo, load_sem.at[1])
    wq_load.start()
    wo_load.start()
    h_load = pltpu.make_async_copy(hidden_hbm, hbuf, load_sem.at[2])

    @pl.when(section == 0)
    def _():
        h_load.start()

    barrier = pltpu.get_barrier_semaphore()

    def greet(s, d):
        pl.semaphore_signal(
            barrier, inc=1, device_id=(s, d), device_id_type=pl.DeviceIdType.MESH
        )

    greet(section, sibling)
    for k in range(1, chips):
        greet(section, peer(k))

    greet((section + 1) % sections, me)
    greet((section + sections - 1) % sections, me)
    pl.semaphore_wait(barrier, chips + 2)

    @pl.when(section == 0)
    def _():
        h_load.wait()

    def h_copy(m):
        return remote(
            out_ref.at[m], hbuf.at[m], h_send.at[m], h_recv.at[m], (section + 1) % sections, me
        )

    def g_copy(m, k):
        slot = gbuf.at[m, me]
        target = sibling if k == 0 else peer(k)
        return remote(slot, slot, g_send.at[m, k], g_recv.at[m, k], section, target)

    def g_arrival(m, k):
        source = sibling if k == 0 else source_chip(k) * 2 + core
        slot = gbuf.at[m, source]
        return remote(slot, slot, g_send.at[m, k], g_recv.at[m, k], section, sibling)

    def f_copy(m, k):
        slot = gbuf.at[m, source_chip(k) * 2 + core]
        return remote(slot, slot, f_send.at[m, k], f_recv.at[m, k], section, sibling)

    def f_arrival(m, k):
        slot = gbuf.at[m, source_chip(k) * 2 + other]
        return remote(slot, slot, f_send.at[m, k], f_recv.at[m, k], section, sibling)

    def r1_copy(m, j):
        return remote(
            pbuf.at[m, other, :, :, pl.ds(j * width, width)],
            r1.at[m, :, :, pl.ds(j * width, width)],
            r1_send.at[m, j],
            r1_recv.at[m, j],
            section,
            sibling,
        )

    def r2_copy(m, j, k):
        return remote(
            tsum.at[m, k, :, pl.ds(j * width, width)],
            r2.at[m, k, :, pl.ds(j * width, width)],
            r2_send.at[m, j, k],
            r2_recv.at[m, j, k],
            section,
            peer(k),
        )

    def begin(m):
        @pl.when(section > 0)
        def _():
            h_copy(m).wait_recv()

        x = hbuf[m].astype(F32)
        moment = jnp.mean(x * x, axis=-1, keepdims=True)
        gbuf[m, me] = (x * lax.rsqrt(moment + 1e-05) * gain_ref[...]).astype(BF16)
        for k in range(1, chips):
            g_copy(m, k).start()
        g_copy(m, 0).start()

    def pass_on(m):
        for k in range(1, chips):
            g_arrival(m, k).wait_recv()
            f_copy(m, k).start()

    def compute(m):
        g_arrival(m, 0).wait_recv()
        for k in range(1, chips):
            f_arrival(m, k).wait_recv()
        x = gbuf[m].reshape(group * mb, features)
        q = (jnp.dot(x, wq[...], preferred_element_type=F32) * scaling).astype(BF16)
        block = (m * mb) // BLOCK_LEN
        heads_out = []
        for h in range(heads):
            ks = slice(h * DH, (h + 1) * DH)
            vs = slice(cols + h * DH, cols + (h + 1) * DH)
            scores = jnp.concatenate(
                [
                    lax.dot_general(
                        q[n * mb : (n + 1) * mb, ks],
                        kv_ref[n * per_dev + block, :, ks],
                        (((1,), (1,)), ((), ())),
                        preferred_element_type=F32,
                    )
                    for n in range(group)
                ],
                axis=0,
            )
            e = jnp.exp(scores - jnp.max(scores, axis=-1, keepdims=True))
            probs = (e / jnp.sum(e, axis=-1, keepdims=True)).astype(BF16)
            heads_out.append(
                jnp.concatenate(
                    [
                        jnp.dot(
                            probs[n * mb : (n + 1) * mb],
                            kv_ref[n * per_dev + block, :, vs],
                            preferred_element_type=F32,
                        )
                        for n in range(group)
                    ],
                    axis=0,
                ).astype(BF16)
            )
        attended = jnp.concatenate(heads_out, axis=1)
        for j in range(CHUNKS):
            at = slice(j * width, (j + 1) * width)
            part = jnp.dot(attended, wo[:, at], preferred_element_type=F32).astype(BF16)
            for n in range(group):
                pbuf[m, n % 2, n // 2, :, at] = part[n * mb : (n + 1) * mb]
            r1_copy(m, j).start()

    def exchange(m):
        for j in range(CHUNKS):
            at = slice(j * width, (j + 1) * width)
            r1_copy(m, j).wait_recv()
            for k in range(1, chips):
                c = (chip + k) % chips
                tsum[m, k, :, at] = (
                    pbuf[m, core, c, :, at].astype(F32) + r1[m, c, :, at].astype(F32)
                ).astype(BF16)
                r2_copy(m, j, k).start()

    def finish(m):
        for j in range(CHUNKS):
            at = slice(j * width, (j + 1) * width)
            total = hbuf[m, :, at].astype(F32)
            total += pbuf[m, core, chip, :, at].astype(F32) + r1[m, chip, :, at].astype(F32)
            for k in range(1, chips):
                r2_copy(m, j, k).wait_recv()
                total += r2[m, k, :, at].astype(F32)
            out_ref[m, :, at] = total.astype(BF16)

        @pl.when(section < sections - 1)
        def _():
            h_copy(m).start()

    begin(0)
    wq_load.wait()
    wo_load.wait()
    pass_on(0)

    def step(m, carry):
        compute(m)

        @pl.when(m + 1 < micro_count)
        def _():
            begin(m + 1)

        exchange(m)

        @pl.when(m + 1 < micro_count)
        def _():
            pass_on(m + 1)

        finish(m)
        return carry

    lax.fori_loop(0, micro_count, step, 0)

    def drain(m, carry):
        for k in range(chips):
            g_copy(m, k).wait_send()
        for k in range(1, chips):
            f_copy(m, k).wait_send()
        for j in range(CHUNKS):
            r1_copy(m, j).wait_send()
            for k in range(1, chips):
                r2_copy(m, j, k).wait_send()

        @pl.when(section < sections - 1)
        def _():
            h_copy(m).wait_send()

        return carry

    lax.fori_loop(0, micro_count, drain, 0)


def per_device(sections, group, hidden, neighbours, norm_gain, w_query, w_kv, w_out):
    tok_rows, features = hidden.shape
    block_count, nbr_length = neighbours.shape[:2]
    cols = w_query.shape[2]
    micro = tok_rows // MB
    chips = group // 2
    pair_weight = w_kv[0].reshape(features, 2 * cols)
    pieces = lax.all_gather(neighbours, "dp", axis=0, tiled=True)
    projected = jnp.dot(
        pieces.reshape(-1, features), pair_weight, preferred_element_type=F32
    ).astype(BF16)
    key_values = projected.reshape(group * block_count, nbr_length, 2 * cols)
    dma = pltpu.SemaphoreType.DMA
    anywhere = pl.BlockSpec(memory_space=pl.ANY)
    vmem = pl.BlockSpec(memory_space=pltpu.VMEM)
    out = pl.pallas_call(
        functools.partial(relay_kernel, sections, group),
        out_shape=jax.ShapeDtypeStruct((micro, MB, features), BF16),
        in_specs=[anywhere, vmem, anywhere, vmem, anywhere],
        out_specs=vmem,
        scratch_shapes=[
            pltpu.VMEM((features, cols), BF16),
            pltpu.VMEM((cols, features), BF16),
            pltpu.VMEM((micro, MB, features), BF16),
            pltpu.VMEM((micro, group, MB, features), BF16),
            pltpu.VMEM((micro, 2, chips, MB, features), BF16),
            pltpu.VMEM((micro, chips, MB, features), BF16),
            pltpu.VMEM((micro, chips, MB, features), BF16),
            pltpu.VMEM((micro, chips, MB, features), BF16),
            dma((3,)),
            dma((micro,)),
            dma((micro,)),
            dma((micro, chips)),
            dma((micro, chips)),
            dma((micro, chips)),
            dma((micro, chips)),
            dma((micro, CHUNKS)),
            dma((micro, CHUNKS)),
            dma((micro, CHUNKS, chips)),
            dma((micro, CHUNKS, chips)),
        ],
        compiler_params=pltpu.CompilerParams(
            collective_id=0, has_side_effects=True, vmem_limit_bytes=60 * 1024 * 1024
        ),
    )(hidden.reshape(micro, MB, features), norm_gain, w_query[0], key_values, w_out[0])
    return out.reshape(1, tok_rows, features)


def solution(mesh):
    placed = (
        P("dp", None),
        P("dp", None, None),
        P("section", None),
        P("section", None, "dp"),
        P("section", None, None, "dp"),
        P("section", "dp", None),
    )
    body = functools.partial(per_device, mesh.shape["section"], mesh.shape["dp"])
    return jax.shard_map(
        body, mesh=mesh, in_specs=placed, out_specs=P("section", "dp", None), check_vma=False
    )
```

```python
import functools
import jax
import jax.numpy as jnp
from jax import lax
from jax.experimental import pallas as pl
from jax.experimental.pallas import tpu as pltpu
from jax.sharding import PartitionSpec as P

DH = 128
BLOCK_LEN = 64
MB = 16
CHUNKS = 2
F32 = jnp.float32
BF16 = jnp.bfloat16


def remote(src, dst, send_sem, recv_sem, section, dp):
    return pltpu.make_async_remote_copy(
        src_ref=src,
        dst_ref=dst,
        send_sem=send_sem,
        recv_sem=recv_sem,
        device_id=(section, dp),
        device_id_type=pl.DeviceIdType.MESH,
    )


def relay_kernel(
    sections,
    group,
    hidden_hbm,
    gain_ref,
    wq_hbm,
    nbr_hbm,
    wkv_hbm,
    wo_hbm,
    out_ref,
    wq,
    wo,
    wkv,
    nbuf,
    kv_ref,
    hbuf,
    gbuf,
    pbuf,
    r1,
    tsum,
    r2,
    load_sem,
    n0_sem,
    n1_send,
    n1_recv,
    n2_send,
    n2_recv,
    n3_send,
    n3_recv,
    h_send,
    h_recv,
    g_send,
    g_recv,
    f_send,
    f_recv,
    r1_send,
    r1_recv,
    r2_send,
    r2_recv,
):
    section = lax.axis_index("section")
    me = lax.axis_index("dp")
    chips = group // 2
    core = me % 2
    chip = me // 2
    other = 1 - core
    sibling = chip * 2 + other
    micro_count, mb, features = hbuf.shape
    cols = wq.shape[1]
    heads = cols // DH
    blocks, nbr_length = kv_ref.shape[2:4]
    pieces = nbuf.shape[2]
    width = features // CHUNKS
    scaling = DH ** (-0.5)

    def peer(k):
        return ((chip + k) % chips) * 2 + core

    def source_chip(k):
        return (chip + chips - k) % chips

    wq_load = pltpu.make_async_copy(wq_hbm, wq, load_sem.at[0])
    wo_load = pltpu.make_async_copy(wo_hbm, wo, load_sem.at[1])
    wkv_load = pltpu.make_async_copy(wkv_hbm, wkv, load_sem.at[3])
    n_load = pltpu.make_async_copy(nbr_hbm, nbuf.at[chip, core], load_sem.at[4])
    n_load.start()
    wkv_load.start()
    wq_load.start()
    wo_load.start()
    h_load = pltpu.make_async_copy(hidden_hbm, hbuf, load_sem.at[2])

    @pl.when(section == 0)
    def _():
        h_load.start()

    barrier = pltpu.get_barrier_semaphore()

    def greet(s, d):
        pl.semaphore_signal(
            barrier, inc=1, device_id=(s, d), device_id_type=pl.DeviceIdType.MESH
        )

    greet(section, sibling)
    for k in range(1, chips):
        greet(section, peer(k))

    for j in range(1, sections):
        greet((section + j) % sections, me)
    pl.semaphore_wait(barrier, chips + sections - 1)

    def n0_copy():
        return remote(
            nbr_hbm, nbuf.at[chip, core], n0_sem.at[0], n0_sem.at[1], section, sibling
        )

    def n0_arrival():
        slot = nbuf.at[chip, other]
        return remote(slot, slot, n0_sem.at[0], n0_sem.at[1], section, sibling)

    def n1_copy(k):
        return remote(
            nbr_hbm.at[section],
            nbuf.at[chip, core, section],
            n1_send.at[k],
            n1_recv.at[k],
            section,
            peer(k),
        )

    def n1_arrival(k):
        slot = nbuf.at[source_chip(k), core, section]
        return remote(slot, slot, n1_send.at[k], n1_recv.at[k], section, sibling)

    def n2_copy(k, j):
        slot = nbuf.at[source_chip(k), core, section]
        return remote(
            slot, slot, n2_send.at[k, j], n2_recv.at[k, j], (section + j) % sections, me
        )

    def n2_arrival(k, j):
        slot = nbuf.at[source_chip(k), core, (section + sections - j) % sections]
        return remote(slot, slot, n2_send.at[k, j], n2_recv.at[k, j], section, sibling)

    def n3_copy(k, j):
        slot = nbuf.at[source_chip(k), core, (section + sections - j) % sections]
        return remote(slot, slot, n3_send.at[k, j], n3_recv.at[k, j], section, sibling)

    def n3_arrival(k, j):
        slot = nbuf.at[source_chip(k), other, (section + sections - j) % sections]
        return remote(slot, slot, n3_send.at[k, j], n3_recv.at[k, j], section, sibling)

    def project(k):
        c = source_chip(k)
        if k == 0:
            n_load.wait()
            n0_arrival().wait_recv()
        else:
            for j in range(pieces):
                n3_arrival(k, j).wait_recv()
        tile = min(cols, 256)

        def columns(i, carry):
            at = pl.ds(pl.multiple_of(i * tile, tile), tile)
            rows = nbuf[c].reshape(-1, features)
            out = jnp.dot(rows, wkv[:, at], preferred_element_type=F32).astype(BF16)
            kv_ref[c, :, :, :, at] = out.reshape(2, blocks, nbr_length, tile)
            return carry

        lax.fori_loop(0, 2 * cols // tile, columns, 0)

    def spread(k):
        n1_arrival(k).wait_recv()
        for j in range(1, pieces):
            n2_copy(k, j).start()
        n3_copy(k, 0).start()

    def share(k):
        for j in range(1, pieces):
            n2_arrival(k, j).wait_recv()
            n3_copy(k, j).start()

    def h_copy(m):
        return remote(
            out_ref.at[m], hbuf.at[m], h_send.at[m], h_recv.at[m], (section + 1) % sections, me
        )

    def g_copy(m, k):
        slot = gbuf.at[m, me]
        target = sibling if k == 0 else peer(k)
        return remote(slot, slot, g_send.at[m, k], g_recv.at[m, k], section, target)

    def g_arrival(m, k):
        source = sibling if k == 0 else source_chip(k) * 2 + core
        slot = gbuf.at[m, source]
        return remote(slot, slot, g_send.at[m, k], g_recv.at[m, k], section, sibling)

    def f_copy(m, k):
        slot = gbuf.at[m, source_chip(k) * 2 + core]
        return remote(slot, slot, f_send.at[m, k], f_recv.at[m, k], section, sibling)

    def f_arrival(m, k):
        slot = gbuf.at[m, source_chip(k) * 2 + other]
        return remote(slot, slot, f_send.at[m, k], f_recv.at[m, k], section, sibling)

    def r1_copy(m, j):
        return remote(
            pbuf.at[m, other, :, :, pl.ds(j * width, width)],
            r1.at[m, :, :, pl.ds(j * width, width)],
            r1_send.at[m, j],
            r1_recv.at[m, j],
            section,
            sibling,
        )

    def r2_copy(m, j, k):
        return remote(
            tsum.at[m, k, :, pl.ds(j * width, width)],
            r2.at[m, k, :, pl.ds(j * width, width)],
            r2_send.at[m, j, k],
            r2_recv.at[m, j, k],
            section,
            peer(k),
        )

    def begin(m):
        @pl.when(section > 0)
        def _():
            h_copy(m).wait_recv()

        x = hbuf[m].astype(F32)
        moment = jnp.mean(x * x, axis=-1, keepdims=True)
        gbuf[m, me] = (x * lax.rsqrt(moment + 1e-05) * gain_ref[...]).astype(BF16)
        for k in range(1, chips):
            g_copy(m, k).start()
        g_copy(m, 0).start()

    def pass_on(m):
        for k in range(1, chips):
            g_arrival(m, k).wait_recv()
            f_copy(m, k).start()

    def compute(m):
        g_arrival(m, 0).wait_recv()
        for k in range(1, chips):
            f_arrival(m, k).wait_recv()
        x = gbuf[m].reshape(group * mb, features)
        q = (jnp.dot(x, wq[...], preferred_element_type=F32) * scaling).astype(BF16)
        block = 0 if blocks == 1 else (m * mb) // BLOCK_LEN
        heads_out = []
        for h in range(heads):
            ks = slice(h * DH, (h + 1) * DH)
            vs = slice(cols + h * DH, cols + (h + 1) * DH)
            scores = jnp.concatenate(
                [
                    lax.dot_general(
                        q[n * mb : (n + 1) * mb, ks],
                        kv_ref[n // 2, n % 2, block, :, ks],
                        (((1,), (1,)), ((), ())),
                        preferred_element_type=F32,
                    )
                    for n in range(group)
                ],
                axis=0,
            )
            e = jnp.exp(scores - jnp.max(scores, axis=-1, keepdims=True))
            probs = (e / jnp.sum(e, axis=-1, keepdims=True)).astype(BF16)
            heads_out.append(
                jnp.concatenate(
                    [
                        jnp.dot(
                            probs[n * mb : (n + 1) * mb],
                            kv_ref[n // 2, n % 2, block, :, vs],
                            preferred_element_type=F32,
                        )
                        for n in range(group)
                    ],
                    axis=0,
                ).astype(BF16)
            )
        attended = jnp.concatenate(heads_out, axis=1)
        for j in range(CHUNKS):
            at = slice(j * width, (j + 1) * width)
            part = jnp.dot(attended, wo[:, at], preferred_element_type=F32).astype(BF16)
            for n in range(group):
                pbuf[m, n % 2, n // 2, :, at] = part[n * mb : (n + 1) * mb]
            r1_copy(m, j).start()

    def exchange(m):
        for j in range(CHUNKS):
            at = slice(j * width, (j + 1) * width)
            r1_copy(m, j).wait_recv()
            for k in range(1, chips):
                c = (chip + k) % chips
                tsum[m, k, :, at] = (
                    pbuf[m, core, c, :, at].astype(F32) + r1[m, c, :, at].astype(F32)
                ).astype(BF16)
                r2_copy(m, j, k).start()

    def finish(m):
        for j in range(CHUNKS):
            at = slice(j * width, (j + 1) * width)
            total = hbuf[m, :, at].astype(F32)
            total += pbuf[m, core, chip, :, at].astype(F32) + r1[m, chip, :, at].astype(F32)
            for k in range(1, chips):
                r2_copy(m, j, k).wait_recv()
                total += r2[m, k, :, at].astype(F32)
            out_ref[m, :, at] = total.astype(BF16)

        @pl.when(section < sections - 1)
        def _():
            h_copy(m).start()

    for k in range(1, chips):
        n1_copy(k).start()
    n0_copy().start()

    @pl.when(section == 0)
    def _():
        h_load.wait()
        begin(0)

    wkv_load.wait()
    spread(1)
    for k in range(2, chips):
        spread(k)
        if k == 2:
            project(0)
        share(k - 1)
    if chips == 2:
        project(0)
    share(chips - 1)
    for k in range(1, chips):
        project(k)

    @pl.when(section > 0)
    def _():
        begin(0)

    wq_load.wait()
    wo_load.wait()
    pass_on(0)

    def step(m, carry):
        compute(m)

        exchange(m)

        @pl.when(m + 1 < micro_count)
        def _():
            begin(m + 1)

        finish(m)

        @pl.when(m + 1 < micro_count)
        def _():
            pass_on(m + 1)

        return carry

    lax.fori_loop(0, micro_count, step, 0)

    n0_copy().wait_send()
    for k in range(1, chips):
        n1_copy(k).wait_send()
        for j in range(pieces):
            n3_copy(k, j).wait_send()
            if j > 0:
                n2_copy(k, j).wait_send()

    def drain(m, carry):
        for k in range(chips):
            g_copy(m, k).wait_send()
        for k in range(1, chips):
            f_copy(m, k).wait_send()
        for j in range(CHUNKS):
            r1_copy(m, j).wait_send()
            for k in range(1, chips):
                r2_copy(m, j, k).wait_send()

        @pl.when(section < sections - 1)
        def _():
            h_copy(m).wait_send()

        return carry

    lax.fori_loop(0, micro_count, drain, 0)


def per_device(sections, group, hidden, neighbours, norm_gain, w_query, w_kv, w_out):
    tok_rows, features = hidden.shape
    block_count, nbr_length = neighbours.shape[:2]
    cols = w_query.shape[2]
    micro = tok_rows // MB
    chips = group // 2
    pair_weight = w_kv[0].reshape(features, 2 * cols)
    piece_rows = block_count * nbr_length // sections
    dma = pltpu.SemaphoreType.DMA
    anywhere = pl.BlockSpec(memory_space=pl.ANY)
    vmem = pl.BlockSpec(memory_space=pltpu.VMEM)
    out = pl.pallas_call(
        functools.partial(relay_kernel, sections, group),
        out_shape=jax.ShapeDtypeStruct((micro, MB, features), BF16),
        in_specs=[anywhere, vmem, anywhere, anywhere, anywhere, anywhere],
        out_specs=vmem,
        scratch_shapes=[
            pltpu.VMEM((features, cols), BF16),
            pltpu.VMEM((cols, features), BF16),
            pltpu.VMEM((features, 2 * cols), BF16),
            pltpu.VMEM((chips, 2, sections, piece_rows, features), BF16),
            pltpu.VMEM((chips, 2, block_count, nbr_length, 2 * cols), BF16),
            pltpu.VMEM((micro, MB, features), BF16),
            pltpu.VMEM((micro, group, MB, features), BF16),
            pltpu.VMEM((micro, 2, chips, MB, features), BF16),
            pltpu.VMEM((micro, chips, MB, features), BF16),
            pltpu.VMEM((micro, chips, MB, features), BF16),
            pltpu.VMEM((micro, chips, MB, features), BF16),
            dma((5,)),
            dma((2,)),
            dma((chips,)),
            dma((chips,)),
            dma((chips, sections)),
            dma((chips, sections)),
            dma((chips, sections)),
            dma((chips, sections)),
            dma((micro,)),
            dma((micro,)),
            dma((micro, chips)),
            dma((micro, chips)),
            dma((micro, chips)),
            dma((micro, chips)),
            dma((micro, CHUNKS)),
            dma((micro, CHUNKS)),
            dma((micro, CHUNKS, chips)),
            dma((micro, CHUNKS, chips)),
        ],
        compiler_params=pltpu.CompilerParams(
            collective_id=0, has_side_effects=True, vmem_limit_bytes=62 * 1024 * 1024
        ),
    )(
        hidden.reshape(micro, MB, features),
        norm_gain,
        w_query[0],
        neighbours.reshape(sections, piece_rows, features),
        pair_weight,
        w_out[0],
    )
    return out.reshape(1, tok_rows, features)


def solution(mesh):
    placed = (
        P("dp", None),
        P("dp", None, None),
        P("section", None),
        P("section", None, "dp"),
        P("section", None, None, "dp"),
        P("section", "dp", None),
    )
    body = functools.partial(per_device, mesh.shape["section"], mesh.shape["dp"])
    return jax.shard_map(
        body, mesh=mesh, in_specs=placed, out_specs=P("section", "dp", None), check_vma=False
    )
```

```python
import functools
import jax
import jax.numpy as jnp
from jax import lax
from jax.experimental import pallas as pl
from jax.experimental.pallas import tpu as pltpu
from jax.sharding import PartitionSpec as P

DH = 128
BLOCK_LEN = 64
MB = 16
CHUNKS = 2
F32 = jnp.float32
BF16 = jnp.bfloat16


def remote(src, dst, send_sem, recv_sem, section, dp):
    return pltpu.make_async_remote_copy(
        src_ref=src,
        dst_ref=dst,
        send_sem=send_sem,
        recv_sem=recv_sem,
        device_id=(section, dp),
        device_id_type=pl.DeviceIdType.MESH,
    )


def relay_kernel(
    sections,
    group,
    hidden_hbm,
    gain_ref,
    wq_hbm,
    nbr_hbm,
    wkv_hbm,
    wo_hbm,
    out_ref,
    wq,
    wo,
    wkv,
    nbuf,
    kv_ref,
    hbuf,
    gbuf,
    pbuf,
    r1,
    tsum,
    r2,
    load_sem,
    n0_sem,
    n1_send,
    n1_recv,
    n2_send,
    n2_recv,
    n3_send,
    n3_recv,
    h_send,
    h_recv,
    g_send,
    g_recv,
    f_send,
    f_recv,
    r1_send,
    r1_recv,
    r2_send,
    r2_recv,
):
    section = lax.axis_index("section")
    me = lax.axis_index("dp")
    chips = group // 2
    core = me % 2
    chip = me // 2
    other = 1 - core
    sibling = chip * 2 + other
    micro_count, mb, features = hbuf.shape
    cols = wq.shape[1]
    heads = cols // DH
    blocks, nbr_length = kv_ref.shape[2:4]
    pieces = nbuf.shape[2]
    width = features // CHUNKS
    scaling = DH ** (-0.5)

    def peer(k):
        return ((chip + k) % chips) * 2 + core

    def source_chip(k):
        return (chip + chips - k) % chips

    wq_load = pltpu.make_async_copy(wq_hbm, wq, load_sem.at[0])
    wo_load = pltpu.make_async_copy(wo_hbm, wo, load_sem.at[1])
    wkv_load = pltpu.make_async_copy(wkv_hbm, wkv, load_sem.at[3])
    n_load = pltpu.make_async_copy(nbr_hbm, nbuf.at[chip, core], load_sem.at[4])
    n_load.start()
    wkv_load.start()
    wq_load.start()
    wo_load.start()
    h_load = pltpu.make_async_copy(hidden_hbm, hbuf, load_sem.at[2])

    @pl.when(section == 0)
    def _():
        h_load.start()

    barrier = pltpu.get_barrier_semaphore()

    def greet(s, d):
        pl.semaphore_signal(
            barrier, inc=1, device_id=(s, d), device_id_type=pl.DeviceIdType.MESH
        )

    greet(section, sibling)
    for k in range(1, chips):
        greet(section, peer(k))

    for j in range(1, sections):
        greet((section + j) % sections, me)
    pl.semaphore_wait(barrier, chips + sections - 1)

    def n0_copy():
        return remote(
            nbr_hbm, nbuf.at[chip, core], n0_sem.at[0], n0_sem.at[1], section, sibling
        )

    def n0_arrival():
        slot = nbuf.at[chip, other]
        return remote(slot, slot, n0_sem.at[0], n0_sem.at[1], section, sibling)

    def n1_copy(k):
        return remote(
            nbr_hbm.at[section],
            nbuf.at[chip, core, section],
            n1_send.at[k],
            n1_recv.at[k],
            section,
            peer(k),
        )

    def n1_arrival(k):
        slot = nbuf.at[source_chip(k), core, section]
        return remote(slot, slot, n1_send.at[k], n1_recv.at[k], section, sibling)

    def n2_copy(k, j):
        slot = nbuf.at[source_chip(k), core, section]
        return remote(
            slot, slot, n2_send.at[k, j], n2_recv.at[k, j], (section + j) % sections, me
        )

    def n2_arrival(k, j):
        slot = nbuf.at[source_chip(k), core, (section + sections - j) % sections]
        return remote(slot, slot, n2_send.at[k, j], n2_recv.at[k, j], section, sibling)

    def n3_copy(k, j):
        slot = nbuf.at[source_chip(k), core, (section + sections - j) % sections]
        return remote(slot, slot, n3_send.at[k, j], n3_recv.at[k, j], section, sibling)

    def n3_arrival(k, j):
        slot = nbuf.at[source_chip(k), other, (section + sections - j) % sections]
        return remote(slot, slot, n3_send.at[k, j], n3_recv.at[k, j], section, sibling)

    def project(k):
        c = source_chip(k)
        if k == 0:
            n_load.wait()
            n0_arrival().wait_recv()
        else:
            for j in range(pieces):
                n3_arrival(k, j).wait_recv()
        tile = min(cols, 256)

        def columns(i, carry):
            at = pl.ds(pl.multiple_of(i * tile, tile), tile)
            rows = nbuf[c].reshape(-1, features)
            out = jnp.dot(rows, wkv[:, at], preferred_element_type=F32).astype(BF16)
            kv_ref[c, :, :, :, at] = out.reshape(2, blocks, nbr_length, tile)
            return carry

        lax.fori_loop(0, 2 * cols // tile, columns, 0)

    def spread(k):
        n1_arrival(k).wait_recv()
        for j in range(1, pieces):
            n2_copy(k, j).start()
        n3_copy(k, 0).start()

    def share(k):
        for j in range(1, pieces):
            n2_arrival(k, j).wait_recv()
            n3_copy(k, j).start()

    def h_copy(m):
        return remote(
            out_ref.at[m], hbuf.at[m], h_send.at[m], h_recv.at[m], (section + 1) % sections, me
        )

    def g_slot(m, j, source):
        return gbuf.at[m, source, :, pl.ds(j * width, width)]

    def g_copy(m, j, k):
        slot = g_slot(m, j, me)
        target = sibling if k == 0 else peer(k)
        return remote(slot, slot, g_send.at[m, j, k], g_recv.at[m, j, k], section, target)

    def g_arrival(m, j, k):
        slot = g_slot(m, j, sibling if k == 0 else source_chip(k) * 2 + core)
        return remote(slot, slot, g_send.at[m, j, k], g_recv.at[m, j, k], section, sibling)

    def f_copy(m, j, k):
        slot = g_slot(m, j, source_chip(k) * 2 + core)
        return remote(slot, slot, f_send.at[m, j, k], f_recv.at[m, j, k], section, sibling)

    def f_arrival(m, j, k):
        slot = g_slot(m, j, source_chip(k) * 2 + other)
        return remote(slot, slot, f_send.at[m, j, k], f_recv.at[m, j, k], section, sibling)

    def r1_copy(m, j):
        return remote(
            pbuf.at[m, other, :, :, pl.ds(j * width, width)],
            r1.at[m, :, :, pl.ds(j * width, width)],
            r1_send.at[m, j],
            r1_recv.at[m, j],
            section,
            sibling,
        )

    def r2_copy(m, j, k):
        return remote(
            tsum.at[m, k, :, pl.ds(j * width, width)],
            r2.at[m, k, :, pl.ds(j * width, width)],
            r2_send.at[m, j, k],
            r2_recv.at[m, j, k],
            section,
            peer(k),
        )

    def begin(m):
        @pl.when(section > 0)
        def _():
            h_copy(m).wait_recv()

        x = hbuf[m].astype(F32)
        moment = jnp.mean(x * x, axis=-1, keepdims=True)
        gbuf[m, me] = (x * lax.rsqrt(moment + 1e-05) * gain_ref[...]).astype(BF16)
        for j in range(CHUNKS):
            for k in range(1, chips):
                g_copy(m, j, k).start()
            g_copy(m, j, 0).start()

    def pass_on(m, j=0):
        for k in range(1, chips):
            g_arrival(m, j, k).wait_recv()
            f_copy(m, j, k).start()

    def compute(m):
        q = None
        for j in range(CHUNKS):
            g_arrival(m, j, 0).wait_recv()
            for k in range(1, chips):
                f_arrival(m, j, k).wait_recv()
            at = slice(j * width, (j + 1) * width)
            x = gbuf[m, :, :, at].reshape(group * mb, width)
            part = jnp.dot(x, wq[at, :], preferred_element_type=F32)
            q = part if q is None else q + part
            if j + 1 < CHUNKS:
                pass_on(m, j + 1)
        q = (q * scaling).astype(BF16)
        block = 0 if blocks == 1 else (m * mb) // BLOCK_LEN
        heads_out = []
        for h in range(heads):
            ks = slice(h * DH, (h + 1) * DH)
            vs = slice(cols + h * DH, cols + (h + 1) * DH)
            scores = jnp.concatenate(
                [
                    lax.dot_general(
                        q[n * mb : (n + 1) * mb, ks],
                        kv_ref[n // 2, n % 2, block, :, ks],
                        (((1,), (1,)), ((), ())),
                        preferred_element_type=F32,
                    )
                    for n in range(group)
                ],
                axis=0,
            )
            e = jnp.exp(scores - jnp.max(scores, axis=-1, keepdims=True))
            probs = (e / jnp.sum(e, axis=-1, keepdims=True)).astype(BF16)
            heads_out.append(
                jnp.concatenate(
                    [
                        jnp.dot(
                            probs[n * mb : (n + 1) * mb],
                            kv_ref[n // 2, n % 2, block, :, vs],
                            preferred_element_type=F32,
                        )
                        for n in range(group)
                    ],
                    axis=0,
                ).astype(BF16)
            )
        attended = jnp.concatenate(heads_out, axis=1)
        for j in range(CHUNKS):
            at = slice(j * width, (j + 1) * width)
            part = jnp.dot(attended, wo[:, at], preferred_element_type=F32).astype(BF16)
            for n in range(group):
                pbuf[m, n % 2, n // 2, :, at] = part[n * mb : (n + 1) * mb]
            r1_copy(m, j).start()

    def exchange(m):
        for j in range(CHUNKS):
            at = slice(j * width, (j + 1) * width)
            r1_copy(m, j).wait_recv()
            for k in range(1, chips):
                c = (chip + k) % chips
                tsum[m, k, :, at] = (
                    pbuf[m, core, c, :, at].astype(F32) + r1[m, c, :, at].astype(F32)
                ).astype(BF16)
                r2_copy(m, j, k).start()

    def finish(m):
        for j in range(CHUNKS):
            at = slice(j * width, (j + 1) * width)
            total = hbuf[m, :, at].astype(F32)
            total += pbuf[m, core, chip, :, at].astype(F32) + r1[m, chip, :, at].astype(F32)
            for k in range(1, chips):
                r2_copy(m, j, k).wait_recv()
                total += r2[m, k, :, at].astype(F32)
            out_ref[m, :, at] = total.astype(BF16)

        @pl.when(section < sections - 1)
        def _():
            h_copy(m).start()

    for k in range(1, chips):
        n1_copy(k).start()
    n0_copy().start()

    @pl.when(section == 0)
    def _():
        h_load.wait()
        begin(0)

    wkv_load.wait()
    for k in range(1, chips):
        spread(k)
    for k in range(1, chips):
        share(k)
        project(k - 1)

    @pl.when(section == 0)
    def _():
        pass_on(0)

    project(chips - 1)

    @pl.when(section > 0)
    def _():
        begin(0)
        pass_on(0)

    wq_load.wait()
    wo_load.wait()

    def step(m, carry):
        compute(m)

        exchange(m)

        @pl.when(m + 1 < micro_count)
        def _():
            begin(m + 1)

        finish(m)

        @pl.when(m + 1 < micro_count)
        def _():
            pass_on(m + 1)

        return carry

    lax.fori_loop(0, micro_count, step, 0)

    n0_copy().wait_send()
    for k in range(1, chips):
        n1_copy(k).wait_send()
        for j in range(pieces):
            n3_copy(k, j).wait_send()
            if j > 0:
                n2_copy(k, j).wait_send()

    def drain(m, carry):
        for j in range(CHUNKS):
            for k in range(chips):
                g_copy(m, j, k).wait_send()
                if k > 0:
                    f_copy(m, j, k).wait_send()
            r1_copy(m, j).wait_send()
            for k in range(1, chips):
                r2_copy(m, j, k).wait_send()

        @pl.when(section < sections - 1)
        def _():
            h_copy(m).wait_send()

        return carry

    lax.fori_loop(0, micro_count, drain, 0)


def per_device(sections, group, hidden, neighbours, norm_gain, w_query, w_kv, w_out):
    tok_rows, features = hidden.shape
    block_count, nbr_length = neighbours.shape[:2]
    cols = w_query.shape[2]
    micro = tok_rows // MB
    chips = group // 2
    pair_weight = w_kv[0].reshape(features, 2 * cols)
    piece_rows = block_count * nbr_length // sections
    dma = pltpu.SemaphoreType.DMA
    anywhere = pl.BlockSpec(memory_space=pl.ANY)
    vmem = pl.BlockSpec(memory_space=pltpu.VMEM)
    out = pl.pallas_call(
        functools.partial(relay_kernel, sections, group),
        out_shape=jax.ShapeDtypeStruct((micro, MB, features), BF16),
        in_specs=[anywhere, vmem, anywhere, anywhere, anywhere, anywhere],
        out_specs=vmem,
        scratch_shapes=[
            pltpu.VMEM((features, cols), BF16),
            pltpu.VMEM((cols, features), BF16),
            pltpu.VMEM((features, 2 * cols), BF16),
            pltpu.VMEM((chips, 2, sections, piece_rows, features), BF16),
            pltpu.VMEM((chips, 2, block_count, nbr_length, 2 * cols), BF16),
            pltpu.VMEM((micro, MB, features), BF16),
            pltpu.VMEM((micro, group, MB, features), BF16),
            pltpu.VMEM((micro, 2, chips, MB, features), BF16),
            pltpu.VMEM((micro, chips, MB, features), BF16),
            pltpu.VMEM((micro, chips, MB, features), BF16),
            pltpu.VMEM((micro, chips, MB, features), BF16),
            dma((5,)),
            dma((2,)),
            dma((chips,)),
            dma((chips,)),
            dma((chips, sections)),
            dma((chips, sections)),
            dma((chips, sections)),
            dma((chips, sections)),
            dma((micro,)),
            dma((micro,)),
            dma((micro, CHUNKS, chips)),
            dma((micro, CHUNKS, chips)),
            dma((micro, CHUNKS, chips)),
            dma((micro, CHUNKS, chips)),
            dma((micro, CHUNKS)),
            dma((micro, CHUNKS)),
            dma((micro, CHUNKS, chips)),
            dma((micro, CHUNKS, chips)),
        ],
        compiler_params=pltpu.CompilerParams(
            collective_id=0, has_side_effects=True, vmem_limit_bytes=62 * 1024 * 1024
        ),
    )(
        hidden.reshape(micro, MB, features),
        norm_gain,
        w_query[0],
        neighbours.reshape(sections, piece_rows, features),
        pair_weight,
        w_out[0],
    )
    return out.reshape(1, tok_rows, features)


def solution(mesh):
    placed = (
        P("dp", None),
        P("dp", None, None),
        P("section", None),
        P("section", None, "dp"),
        P("section", None, None, "dp"),
        P("section", "dp", None),
    )
    body = functools.partial(per_device, mesh.shape["section"], mesh.shape["dp"])
    return jax.shard_map(
        body, mesh=mesh, in_specs=placed, out_specs=P("section", "dp", None), check_vma=False
    )
```
